32 devices in a mesh: shard: 16 (over z, y, x), tensor: 2 (over core).
Axes of the slice: x: 2, y: 2, z: 4, core: 2. Of those that a mesh axis runs over, the one named last changes fastest.
Arguments:
- step_count: int32 [1], replicated, may hold values from 1 to 100
- attn_side: int32 [4], replicated, may hold values from 0 to 1, as said below
- attn_grad: bfloat16 [4, 2048, 2048], P(None, 'shard', 'tensor'), may hold values from -40 to 40
- gate_grad: bfloat16 [2048, 10944], P('shard', 'tensor'), may hold values from -40 to 40
- down_grad: bfloat16 [10944, 2048], P('shard', 'tensor'), may hold values from -40 to 40
- left_basis: bfloat16 [2, 2048, 256], P(None, 'shard'), may hold values from -0.125 to 0.125
- right_basis: bfloat16 [2, 2048, 256], P(None, 'tensor'), may hold values from -0.125 to 0.125
- gate_basis: bfloat16 [2048, 256], P('shard'), may hold values from -0.125 to 0.125
- down_basis: bfloat16 [2048, 256], P('tensor'), may hold values from -0.125 to 0.125
- left_first: float32 [2, 256, 2048], P(None, 'shard', 'tensor'), may hold values from -6 to 6
- left_second: float32 [2, 256, 2048], P(None, 'shard', 'tensor'), may hold values from 0.01 to 1
- right_first: float32 [2, 2048, 256], P(None, 'shard', 'tensor'), may hold values from -6 to 6
- right_second: float32 [2, 2048, 256], P(None, 'shard', 'tensor'), may hold values from 0.01 to 1
- gate_first: float32 [256, 10944], P('shard', 'tensor'), may hold values from -6 to 6
- gate_second: float32 [256, 10944], P('shard', 'tensor'), may hold values from 0.01 to 1
- down_first: float32 [10944, 256], P('shard', 'tensor'), may hold values from -6 to 6
- down_second: float32 [10944, 256], P('shard', 'tensor'), may hold values from 0.01 to 1
- norm_param: float32 [2, 2048], P(None, ('shard', 'tensor')), may hold values from 0.5 to 1.5
- norm_grad: float32 [2, 2048], P(None, ('shard', 'tensor')), may hold values from -6 to 6
- norm_first: float32 [2, 2048], P(None, ('shard', 'tensor')), may hold values from -6 to 6
- norm_second: float32 [2, 2048], P(None, ('shard', 'tensor')), may hold values from 0.01 to 1
Outputs:
- attn_update: float32 [4, 2048, 2048], P(None, 'shard', 'tensor')
- gate_update: float32 [2048, 10944], P('shard', 'tensor')
- down_update: float32 [10944, 2048], P('shard', 'tensor')
- left_first_new: float32 [2, 256, 2048], P(None, 'shard', 'tensor')
- left_second_new: float32 [2, 256, 2048], P(None, 'shard', 'tensor')
- right_first_new: float32 [2, 2048, 256], P(None, 'shard', 'tensor')
- right_second_new: float32 [2, 2048, 256], P(None, 'shard', 'tensor')
- gate_first_new: float32 [256, 10944], P('shard', 'tensor')
- gate_second_new: float32 [256, 10944], P('shard', 'tensor')
- down_first_new: float32 [10944, 256], P('shard', 'tensor')
- down_second_new: float32 [10944, 256], P('shard', 'tensor')
- left_basis_new: bfloat16 [2, 2048, 256], P(None, ('shard', 'tensor'))
- right_basis_new: bfloat16 [2, 2, 1024, 256], P(None, 'tensor', 'shard')
- gate_basis_new: bfloat16 [2048, 256], P(('shard', 'tensor'))
- down_basis_new: bfloat16 [2, 1024, 256], P('tensor', 'shard')
- norm_param_new: float32 [2, 2048], P(None, ('shard', 'tensor'))
- norm_first_new: float32 [2, 2048], P(None, ('shard', 'tensor'))
- norm_second_new: float32 [2, 2048], P(None, ('shard', 'tensor'))
The draws below stay inside these ranges and needn't reach their ends.
Inputs may be any that keep to these rules, and one draw needn't show every extreme that they name: `attn_side`: exactly two of the four attention matrices take each side.
All inputs are finite; a program needn't handle non-finite values.
Results may differ from the reference program's by a relative error of at most 0.004.
Values may be sent and summed in bfloat16 or wider, within the bound.
No kernel may reach another device: no remote copies, remote signals or barrier semaphores. Data moves between devices by JAX's collectives and lax.ppermute only.
A program may use at most 128 MiB of HBM per device.

```python
import math
import jax
import jax.numpy as jnp
from jax import lax

D = 2048
FF = 10944
RANK = 256
NSITER = 5
N_TENSOR = 2


def scaled_field(key, stack_count, row_count, col_count):
    key_rows, key_cols, key_values = jax.random.split(key, 3)
    row_place = jnp.arange(row_count, dtype=jnp.float32)[None, :, None] / row_count
    col_place = jnp.arange(col_count, dtype=jnp.float32)[None, None, :] / col_count
    row_scale = 3.0 ** (row_place - 0.5) * 10.0 ** (0.5 * jax.random.uniform(key_rows, (stack_count, row_count, 1), dtype=jnp.float32) - 0.25)
    col_scale = 3.0 ** (col_place - 0.5) * 10.0 ** (0.5 * jax.random.uniform(key_cols, (stack_count, 1, col_count), dtype=jnp.float32) - 0.25)
    values = jax.random.truncated_normal(key_values, -4.0, 4.0, (stack_count, row_count, col_count), dtype=jnp.float32)
    return values * row_scale * col_scale


def draw_attn_side(key, part):
    own_key = jax.random.fold_in(key, 11)
    return jax.random.permutation(own_key, jnp.array([0, 0, 1, 1], dtype=jnp.int32))


def draw_attn_grad(key, part):
    own_key = jax.random.fold_in(key, 23)
    return scaled_field(own_key, 4, D, D).astype(jnp.bfloat16)


def draw_gate_grad(key, part):
    own_key = jax.random.fold_in(key, 37)
    return scaled_field(own_key, 1, D, FF)[0].astype(jnp.bfloat16)


def draw_down_grad(key, part):
    own_key = jax.random.fold_in(key, 53)
    return scaled_field(own_key, 1, FF, D)[0].astype(jnp.bfloat16)


def block_levels(key, shape, shards, least, top_value):
    def one(axis_at, blocks):
        heights = jax.random.uniform(jax.random.fold_in(jax.random.fold_in(key, 6), axis_at), (blocks,), jnp.float32, least / len(shards), top_value / len(shards))
        return jnp.repeat(jnp.exp(heights), shape[axis_at] // blocks).reshape((-1,) + (1,) * (len(shape) - axis_at - 1))

    level = one(*shards[0])
    for cut in shards[1:]:
        level = level * one(*cut)
    return level


def normal_values(stream_key, shape, width, most, cuts=(), kind=jnp.bfloat16):
    factor_of = block_levels(stream_key, shape, cuts, -0.22, 0.18) if cuts else 1.0
    values = jax.random.normal(stream_key, shape, jnp.float32) * width * factor_of
    return jnp.minimum(jnp.maximum(values, -most), most).astype(kind)


def setup_inputs(seed: int = 0) -> dict:
    keys = jax.random.split(jax.random.key(seed), 22)
    step_count = jax.random.randint(keys[0], (1,), 1, 101).astype(jnp.int32)
    attn_side = draw_attn_side(jax.random.fold_in(keys[21], 71), 0)
    attn_grad = draw_attn_grad(jax.random.fold_in(keys[21], 71), 0)
    gate_grad = draw_gate_grad(jax.random.fold_in(keys[21], 71), 0)
    down_grad = draw_down_grad(jax.random.fold_in(keys[21], 71), 0)
    left_basis = normal_values(keys[5], (2, D, RANK), D ** -0.5, 0.125, ((1, 16),))
    right_basis = normal_values(keys[6], (2, D, RANK), D ** -0.5, 0.125, ((1, 2),))
    gate_basis = normal_values(keys[7], (D, RANK), D ** -0.5, 0.125, ((0, 16),))
    down_basis = normal_values(keys[8], (D, RANK), D ** -0.5, 0.125, ((0, 2),))
    left_first = normal_values(keys[9], (2, RANK, D), 1.0, 6.0, ((1, 16), (2, 2)), jnp.float32)
    left_second = jnp.clip(jnp.exp(math.log(1.0) - 4.6051702 * jax.random.uniform(keys[10], (2, RANK, D), jnp.float32) ** block_levels(keys[10], (2, RANK, D), ((1, 16), (2, 2)), -0.2, 0.2)), 0.01, 1.0)
    right_first = normal_values(keys[11], (2, D, RANK), 1.0, 6.0, ((1, 16), (2, 2)), jnp.float32)
    right_second = jnp.clip(jnp.exp(math.log(1.0) - 4.6051702 * jax.random.uniform(keys[12], (2, D, RANK), jnp.float32) ** block_levels(keys[12], (2, D, RANK), ((1, 16), (2, 2)), -0.2, 0.2)), 0.01, 1.0)
    gate_first = normal_values(keys[13], (RANK, FF), 1.0, 6.0, ((0, 16), (1, 2)), jnp.float32)
    gate_second = jnp.clip(jnp.exp(math.log(1.0) - 4.6051702 * jax.random.uniform(keys[14], (RANK, FF), jnp.float32) ** block_levels(keys[14], (RANK, FF), ((0, 16), (1, 2)), -0.2, 0.2)), 0.01, 1.0)
    down_first = normal_values(keys[15], (FF, RANK), 1.0, 6.0, ((0, 16), (1, 2)), jnp.float32)
    down_second = jnp.clip(jnp.exp(math.log(1.0) - 4.6051702 * jax.random.uniform(keys[16], (FF, RANK), jnp.float32) ** block_levels(keys[16], (FF, RANK), ((0, 16), (1, 2)), -0.2, 0.2)), 0.01, 1.0)
    norm_param = jnp.clip(1.0 + 0.1 * jax.random.normal(keys[17], (2, D), jnp.float32), 0.5, 1.5)
    norm_grad = normal_values(keys[18], (2, D), 1.0, 6.0, ((1, 32),), jnp.float32)
    norm_first = normal_values(keys[19], (2, D), 0.5, 6.0, ((1, 32),), jnp.float32)
    norm_second = jnp.clip(jnp.exp(math.log(1.0) - 4.6051702 * jax.random.uniform(keys[20], (2, D), jnp.float32) ** block_levels(keys[20], (2, D), ((1, 32),), -0.2, 0.2)), 0.01, 1.0)
    return dict(step_count=step_count, attn_side=attn_side, attn_grad=attn_grad, gate_grad=gate_grad, down_grad=down_grad, left_basis=left_basis, right_basis=right_basis, gate_basis=gate_basis, down_basis=down_basis, left_first=left_first, left_second=left_second, right_first=right_first, right_second=right_second, gate_first=gate_first, gate_second=gate_second, down_first=down_first, down_second=down_second, norm_param=norm_param, norm_grad=norm_grad, norm_first=norm_first, norm_second=norm_second)


highest = lax.Precision.HIGHEST
beta_one = 0.9
beta_two = 0.999
adam_eps = 1e-08
galore_scale = 0.25
norm_rate = 0.001
weight_decay = 0.1

def adam_moments(gradient, first_moment, second_moment, step_float):
    first_new = beta_one * first_moment + (1.0 - beta_one) * gradient
    second_new = beta_two * second_moment + (1.0 - beta_two) * gradient * gradient
    corr_first = 1.0 - beta_one ** step_float
    corr_second = 1.0 - beta_two ** step_float
    direction = first_new / corr_first / (jnp.sqrt(second_new / corr_second) + adam_eps)
    return (first_new, second_new, direction)

def polar_factor(subspace):
    sum_squares = jnp.sum(subspace * subspace)
    normed = subspace / jnp.sqrt(sum_squares)
    identity = jnp.eye(subspace.shape[1], dtype=subspace.dtype)
    for turn_index in range(NSITER):
        gram_matrix = jnp.dot(normed.T, normed, precision=highest)
        normed = jnp.dot(normed, 1.5 * identity - 0.5 * gram_matrix, precision=highest)
    return normed.astype(jnp.bfloat16)

def left_side(gradient, base_matrix, first_moment, second_moment, step_float):
    projected = jnp.dot(base_matrix.T, gradient, preferred_element_type=jnp.float32)
    first_new, second_new, direction = adam_moments(projected, first_moment, second_moment, step_float)
    update = galore_scale * jnp.dot(base_matrix, direction.astype(jnp.bfloat16), preferred_element_type=jnp.float32)
    subspace = jnp.dot(gradient, projected.astype(jnp.bfloat16).T, preferred_element_type=jnp.float32)
    return (update, first_new, second_new, polar_factor(subspace))

def right_side(gradient, base_matrix, first_moment, second_moment, step_float):
    projected = jnp.dot(gradient, base_matrix, preferred_element_type=jnp.float32)
    first_new, second_new, direction = adam_moments(projected, first_moment, second_moment, step_float)
    update = galore_scale * jnp.dot(direction.astype(jnp.bfloat16), base_matrix.T, preferred_element_type=jnp.float32)
    subspace = jnp.dot(gradient.T, projected.astype(jnp.bfloat16), preferred_element_type=jnp.float32)
    return (update, first_new, second_new, polar_factor(subspace))

def reference(step_count, attn_side, attn_grad, gate_grad, down_grad, left_basis, right_basis, gate_basis, down_basis, left_first, left_second, right_first, right_second, gate_first, gate_second, down_first, down_second, norm_param, norm_grad, norm_first, norm_second):
    step_float = step_count[0].astype(jnp.float32)
    ordering = jnp.argsort(attn_side, stable=True).astype(jnp.int32)
    inverse = jnp.argsort(ordering, stable=True).astype(jnp.int32)
    updates = []
    left_firsts, left_seconds, left_bases = ([], [], [])
    for slot in range(2):
        result = left_side(attn_grad[ordering[slot]], left_basis[slot], left_first[slot], left_second[slot], step_float)
        updates.append(result[0])
        left_firsts.append(result[1])
        left_seconds.append(result[2])
        left_bases.append(result[3])
    right_firsts, right_seconds, right_bases = ([], [], [])
    for slot in range(2):
        result = right_side(attn_grad[ordering[2 + slot]], right_basis[slot], right_first[slot], right_second[slot], step_float)
        updates.append(result[0])
        right_firsts.append(result[1])
        right_seconds.append(result[2])
        right_bases.append(result[3].reshape(N_TENSOR, D // N_TENSOR, RANK))
    attn_update = jnp.take(jnp.stack(updates), inverse, axis=0)
    gate_update, gate_first_new, gate_second_new, gate_basis_new = left_side(gate_grad, gate_basis, gate_first, gate_second, step_float)
    down_update, down_first_new, down_second_new, down_new = right_side(down_grad, down_basis, down_first, down_second, step_float)
    norm_first_new, norm_second_new, norm_direction = adam_moments(norm_grad, norm_first, norm_second, step_float)
    norm_param_new = norm_param - norm_rate * (norm_direction + weight_decay * norm_param)
    return (attn_update, gate_update, down_update, jnp.stack(left_firsts), jnp.stack(left_seconds), jnp.stack(right_firsts), jnp.stack(right_seconds), gate_first_new, gate_second_new, down_first_new, down_second_new, jnp.stack(left_bases), jnp.stack(right_bases), gate_basis_new, down_new.reshape(N_TENSOR, D // N_TENSOR, RANK), norm_param_new, norm_first_new, norm_second_new)
```

```python
import functools

import jax
import jax.numpy as jnp
from jax import lax
from jax.sharding import PartitionSpec as P

NSITER = 5


highest = lax.Precision.HIGHEST
beta_one = 0.9
beta_two = 0.999
adam_eps = 1e-08
galore_scale = 0.25
norm_rate = 0.001
weight_decay = 0.1


def adam_moments(gradient, first_moment, second_moment, step_float):
    first_new = beta_one * first_moment + (1.0 - beta_one) * gradient
    second_new = beta_two * second_moment + (1.0 - beta_two) * gradient * gradient
    corr_first = 1.0 - beta_one**step_float
    corr_second = 1.0 - beta_two**step_float
    direction = first_new / corr_first / (jnp.sqrt(second_new / corr_second) + adam_eps)
    return (first_new, second_new, direction)


def batch_product(first_factor, second_factor):
    return jnp.einsum("kij,kjl->kil", first_factor, second_factor, precision=highest)


def swap_sum(parts, axis_name, size):
    if size == 1:
        return parts[0]
    if size == 2:
        own = lax.axis_index(axis_name)
        mine = lax.dynamic_index_in_dim(parts, own, 0, keepdims=False)
        other = lax.dynamic_index_in_dim(parts, 1 - own, 0, keepdims=False)
        return mine + lax.ppermute(other, axis_name, [(0, 1), (1, 0)])
    return jnp.sum(lax.all_to_all(parts, axis_name, 0, 0), axis=0)


def exchange_sum(parts, axis_name):
    received = lax.all_to_all(parts.astype(jnp.bfloat16), axis_name, 0, 0)
    return jnp.sum(received.astype(jnp.float32), axis=0)


def split_at(array, axis, count):
    shape = array.shape[:axis] + (count, array.shape[axis] // count) + array.shape[axis + 1 :]
    return jnp.moveaxis(array.reshape(shape), axis, 0)


def body(
    n_shard,
    n_tensor,
    step_count,
    attn_side,
    attn_grad,
    gate_grad,
    down_grad,
    left_basis,
    right_basis,
    gate_basis,
    down_basis,
    left_first,
    left_second,
    right_first,
    right_second,
    gate_first,
    gate_second,
    down_first,
    down_second,
    norm_param,
    norm_grad,
    norm_first,
    norm_second,
):
    step_float = step_count[0].astype(jnp.float32)
    ordering = jnp.argsort(attn_side, stable=True)
    inverse = jnp.argsort(ordering, stable=True)
    picked = jnp.take(attn_grad, ordering, axis=0)
    left_grad = picked[:2]
    right_grad = picked[2:]
    bf16 = jnp.bfloat16
    f32 = jnp.float32
    columns = left_grad.shape[2]
    left_part = jnp.concatenate(
        [
            jnp.dot(left_basis[0].T, left_grad[0], preferred_element_type=f32).astype(bf16),
            jnp.dot(left_basis[1].T, left_grad[1], preferred_element_type=f32).astype(bf16),
            jnp.dot(gate_basis.T, gate_grad, preferred_element_type=f32).astype(bf16),
        ],
        axis=1,
    )
    projected = exchange_sum(split_at(left_part, 0, n_shard), "shard")
    rounded = projected.astype(bf16)
    proj_all = lax.all_gather(rounded, "shard", axis=0, tiled=True)
    left_projected = jnp.stack([projected[:, :columns], projected[:, columns : 2 * columns]])
    gate_projected = projected[:, 2 * columns :]
    left_first_new, left_second_new, left_direction = adam_moments(
        left_projected, left_first, left_second, step_float
    )
    gate_first_new, gate_second_new, gate_direction = adam_moments(
        gate_projected, gate_first, gate_second, step_float
    )
    direction = jnp.concatenate(
        [
            left_direction[0].astype(bf16),
            left_direction[1].astype(bf16),
            gate_direction.astype(bf16),
        ],
        axis=1,
    )
    dir_all = lax.all_gather(direction, "shard", axis=0, tiled=True)

    right_part = jnp.einsum("kmn,knr->kmr", right_grad, right_basis, preferred_element_type=f32)
    down_part = jnp.dot(down_grad, down_basis, preferred_element_type=f32)
    right_projected = swap_sum(split_at(right_part, 2, n_tensor), "tensor", n_tensor)
    down_projected = swap_sum(split_at(down_part, 1, n_tensor), "tensor", n_tensor)
    right_first_new, right_second_new, right_direction = adam_moments(
        right_projected, right_first, right_second, step_float
    )
    down_first_new, down_second_new, down_direction = adam_moments(
        down_projected, down_first, down_second, step_float
    )
    right_dir_all, down_dir_all, right_proj_all, down_proj_all = (
        lax.all_gather(right_direction.astype(bf16), "tensor", axis=2, tiled=True),
        lax.all_gather(down_direction.astype(bf16), "tensor", axis=1, tiled=True),
        lax.all_gather(right_projected.astype(bf16), "tensor", axis=2, tiled=True),
        lax.all_gather(down_projected.astype(bf16), "tensor", axis=1, tiled=True),
    )
    right_sub_part = jnp.einsum(
        "kmn,kmr->knr", right_grad, right_proj_all, preferred_element_type=f32
    )
    down_sub_part = jnp.einsum("mn,mr->nr", down_grad, down_proj_all, preferred_element_type=f32)
    right_parts = jnp.concatenate([right_sub_part, down_sub_part[None]], axis=0)
    right_sub = exchange_sum(split_at(right_parts, 1, n_shard), "shard")
    right_update = galore_scale * jnp.einsum(
        "kmr,knr->kmn", right_dir_all, right_basis, preferred_element_type=f32
    )
    down_update = galore_scale * jnp.einsum(
        "mr,nr->mn", down_dir_all, down_basis, preferred_element_type=f32
    )

    left_sub_part = jnp.stack(
        [
            jnp.einsum(
                "mn,rn->mr", left_grad[0], proj_all[:, :columns], preferred_element_type=f32
            ),
            jnp.einsum(
                "mn,rn->mr",
                left_grad[1],
                proj_all[:, columns : 2 * columns],
                preferred_element_type=f32,
            ),
            jnp.einsum(
                "mn,rn->mr", gate_grad, proj_all[:, 2 * columns :], preferred_element_type=f32
            ),
        ]
    )
    left_sub = swap_sum(split_at(left_sub_part, 1, n_tensor), "tensor", n_tensor)
    subspace = jnp.concatenate([left_sub, right_sub], axis=0)
    rank_width = subspace.shape[2]
    count = subspace.shape[0]
    gram_part = jnp.einsum("kir,kis->krs", subspace, subspace, precision=highest)
    gram_parts = gram_part.reshape(n_tensor, n_shard, -1, rank_width)
    gram_block = exchange_sum(swap_sum(gram_parts, "tensor", n_tensor), "shard")
    spread = lax.all_to_all(
        jnp.broadcast_to(gram_block.astype(bf16)[None], (n_shard,) + gram_block.shape),
        "shard",
        0,
        0,
    )
    gram_raw = lax.all_gather(spread, "tensor", axis=0, tiled=False)
    gram_raw = gram_raw.reshape(count, rank_width, rank_width).astype(f32)
    identity = jnp.eye(rank_width, dtype=f32)
    sum_squares = jnp.sum(gram_raw * identity, axis=(1, 2))
    gram_matrix = gram_raw / sum_squares[:, None, None]
    mixing = identity
    for turn_index in range(NSITER):
        factor = 1.5 * identity - 0.5 * gram_matrix
        if turn_index == 0:
            mixing = factor
        else:
            mixing = batch_product(mixing, factor)
        if turn_index + 1 < NSITER:
            gram_matrix = batch_product(batch_product(factor, factor), gram_matrix)
    normed = subspace / jnp.sqrt(sum_squares)[:, None, None]
    refreshed = batch_product(normed, mixing).astype(bf16)

    left_update = galore_scale * jnp.stack(
        [
            jnp.dot(left_basis[0], dir_all[:, :columns], preferred_element_type=f32),
            jnp.dot(left_basis[1], dir_all[:, columns : 2 * columns], preferred_element_type=f32),
        ]
    )
    gate_update = galore_scale * jnp.dot(
        gate_basis, dir_all[:, 2 * columns :], preferred_element_type=f32
    )
    attn_update = jnp.take(jnp.concatenate([left_update, right_update], axis=0), inverse, axis=0)
    norm_first_new, norm_second_new, norm_direction = adam_moments(
        norm_grad, norm_first, norm_second, step_float
    )
    norm_param_new = norm_param - norm_rate * (norm_direction + weight_decay * norm_param)
    return (
        attn_update,
        gate_update,
        down_update,
        left_first_new,
        left_second_new,
        right_first_new,
        right_second_new,
        gate_first_new,
        gate_second_new,
        down_first_new,
        down_second_new,
        refreshed[0:2],
        refreshed[3:5][:, None],
        refreshed[2],
        refreshed[5][None],
        norm_param_new,
        norm_first_new,
        norm_second_new,
    )


def solution(mesh):
    in_specs = (
        P(),
        P(),
        P(None, "shard", "tensor"),
        P("shard", "tensor"),
        P("shard", "tensor"),
        P(None, "shard", None),
        P(None, "tensor", None),
        P("shard", None),
        P("tensor", None),
        P(None, "shard", "tensor"),
        P(None, "shard", "tensor"),
        P(None, "shard", "tensor"),
        P(None, "shard", "tensor"),
        P("shard", "tensor"),
        P("shard", "tensor"),
        P("shard", "tensor"),
        P("shard", "tensor"),
        P(None, ("shard", "tensor")),
        P(None, ("shard", "tensor")),
        P(None, ("shard", "tensor")),
        P(None, ("shard", "tensor")),
    )
    out_specs = (
        P(None, "shard", "tensor"),
        P("shard", "tensor"),
        P("shard", "tensor"),
        P(None, "shard", "tensor"),
        P(None, "shard", "tensor"),
        P(None, "shard", "tensor"),
        P(None, "shard", "tensor"),
        P("shard", "tensor"),
        P("shard", "tensor"),
        P("shard", "tensor"),
        P("shard", "tensor"),
        P(None, ("shard", "tensor"), None),
        P(None, "tensor", "shard", None),
        P(("shard", "tensor"), None),
        P("tensor", "shard", None),
        P(None, ("shard", "tensor")),
        P(None, ("shard", "tensor")),
        P(None, ("shard", "tensor")),
    )
    return jax.shard_map(
        functools.partial(body, mesh.shape["shard"], mesh.shape["tensor"]),
        mesh=mesh, in_specs=in_specs, out_specs=out_specs, check_vma=False)
```

```python
import functools

import jax
import jax.numpy as jnp
from jax import lax
from jax.sharding import PartitionSpec as P

NSITER = 5


highest = lax.Precision.HIGHEST
beta_one = 0.9
beta_two = 0.999
adam_eps = 1e-08
galore_scale = 0.25
norm_rate = 0.001
weight_decay = 0.1


def adam_moments(gradient, first_moment, second_moment, step_float):
    first_new = beta_one * first_moment + (1.0 - beta_one) * gradient
    second_new = beta_two * second_moment + (1.0 - beta_two) * gradient * gradient
    corr_first = 1.0 - beta_one**step_float
    corr_second = 1.0 - beta_two**step_float
    direction = first_new / corr_first / (jnp.sqrt(second_new / corr_second) + adam_eps)
    return (first_new, second_new, direction)


def batch_product(first_factor, second_factor):
    return jnp.einsum("kij,kjl->kil", first_factor, second_factor, precision=highest)


def swap_sum(parts, axis_name, size):
    if size == 1:
        return parts[0]
    if size == 2:
        own = lax.axis_index(axis_name)
        mine = lax.dynamic_index_in_dim(parts, own, 0, keepdims=False)
        other = lax.dynamic_index_in_dim(parts, 1 - own, 0, keepdims=False)
        return mine + lax.ppermute(other, axis_name, [(0, 1), (1, 0)])
    return jnp.sum(lax.all_to_all(parts, axis_name, 0, 0), axis=0)


def exchange_sum(parts, axis_name):
    received = lax.all_to_all(parts.astype(jnp.bfloat16), axis_name, 0, 0)
    return jnp.sum(received.astype(jnp.float32), axis=0)


def lane_matrix(order, count, block, axis_name):
    place = lax.iota(jnp.int32, count)
    relative = jnp.zeros_like(place)
    for level, bit in enumerate(order):
        relative = relative | (((place >> (len(order) - 1 - level)) & 1) << bit)
    start = (lax.axis_index(axis_name) ^ relative) * block
    target = (start[:, None] + lax.iota(jnp.int32, block)[None]).reshape(count * block, 1)
    return (target == lax.iota(jnp.int32, count * block)[None]).astype(jnp.bfloat16)


def partners(bit, count):
    return [(index, index ^ (1 << bit)) for index in range(count)]


def lane_reduce(part, order, count, axis_name):
    for bit in order:
        half = part.shape[0] // 2
        other = lax.ppermute(part[half:].astype(jnp.bfloat16), axis_name, partners(bit, count))
        part = part[:half] + other.astype(jnp.float32)
    return part


def lane_gather(block, order, count, axis_name):
    for bit in reversed(order):
        other = lax.ppermute(block, axis_name, partners(bit, count))
        block = jnp.concatenate([block, other], axis=0)
    return block


def split_at(array, axis, count):
    shape = array.shape[:axis] + (count, array.shape[axis] // count) + array.shape[axis + 1 :]
    return jnp.moveaxis(array.reshape(shape), axis, 0)


def body(
    n_shard,
    n_tensor,
    step_count,
    attn_side,
    attn_grad,
    gate_grad,
    down_grad,
    left_basis,
    right_basis,
    gate_basis,
    down_basis,
    left_first,
    left_second,
    right_first,
    right_second,
    gate_first,
    gate_second,
    down_first,
    down_second,
    norm_param,
    norm_grad,
    norm_first,
    norm_second,
):
    step_float = step_count[0].astype(jnp.float32)
    ordering = jnp.argsort(attn_side, stable=True)
    inverse = jnp.argsort(ordering, stable=True)
    picked = jnp.take(attn_grad, ordering, axis=0)
    left_grad = picked[:2]
    right_grad = picked[2:]
    bf16 = jnp.bfloat16
    f32 = jnp.float32
    columns = left_grad.shape[2]
    rank_width = gate_basis.shape[1]
    block = rank_width // n_shard
    bits = list(range(n_shard.bit_length() - 1))
    orders = (bits[2:] + bits[:2], bits, bits[1::-1] + bits[2:])
    lanes = [lane_matrix(order, n_shard, block, "shard") for order in orders]
    gate_columns = gate_grad.shape[1]
    cut = max(gate_columns // 256 * 128, 1)
    gate_pieces = (gate_grad[:, :cut], gate_grad[:, cut:])
    left_lane_basis = jnp.einsum("kmr,pr->kmp", left_basis, lanes[0])
    gate_lane_basis = [jnp.einsum("mr,pr->mp", gate_basis, lane) for lane in lanes[1:]]
    parts = [
        jnp.concatenate(
            [
                jnp.dot(left_lane_basis[0].T, left_grad[0], preferred_element_type=f32),
                jnp.dot(left_lane_basis[1].T, left_grad[1], preferred_element_type=f32),
            ],
            axis=1,
        ),
        jnp.dot(gate_lane_basis[0].T, gate_pieces[0], preferred_element_type=f32),
        jnp.dot(gate_lane_basis[1].T, gate_pieces[1], preferred_element_type=f32),
    ]
    summed = [lane_reduce(part, order, n_shard, "shard") for part, order in zip(parts, orders)]
    proj_all = [
        lane_gather(piece.astype(bf16), order, n_shard, "shard")
        for piece, order in zip(summed, orders)
    ]
    left_projected = jnp.stack([summed[0][:, :columns], summed[0][:, columns:]])
    gate_projected = jnp.concatenate(summed[1:], axis=1)
    left_first_new, left_second_new, left_direction = adam_moments(
        left_projected, left_first, left_second, step_float
    )
    gate_first_new, gate_second_new, gate_direction = adam_moments(
        gate_projected, gate_first, gate_second, step_float
    )
    directions = [
        jnp.concatenate([left_direction[0].astype(bf16), left_direction[1].astype(bf16)], axis=1),
        gate_direction[:, :cut].astype(bf16),
        gate_direction[:, cut:].astype(bf16),
    ]
    dir_all = [
        lane_gather(piece, order, n_shard, "shard") for piece, order in zip(directions, orders)
    ]

    right_part = jnp.einsum("kmn,knr->kmr", right_grad, right_basis, preferred_element_type=f32)
    down_part = jnp.dot(down_grad, down_basis, preferred_element_type=f32)
    right_projected = swap_sum(split_at(right_part, 2, n_tensor), "tensor", n_tensor)
    down_projected = swap_sum(split_at(down_part, 1, n_tensor), "tensor", n_tensor)
    right_first_new, right_second_new, right_direction = adam_moments(
        right_projected, right_first, right_second, step_float
    )
    down_first_new, down_second_new, down_direction = adam_moments(
        down_projected, down_first, down_second, step_float
    )
    right_dir_all, down_dir_all, right_proj_all, down_proj_all = (
        lax.all_gather(right_direction.astype(bf16), "tensor", axis=2, tiled=True),
        lax.all_gather(down_direction.astype(bf16), "tensor", axis=1, tiled=True),
        lax.all_gather(right_projected.astype(bf16), "tensor", axis=2, tiled=True),
        lax.all_gather(down_projected.astype(bf16), "tensor", axis=1, tiled=True),
    )
    right_sub_part = jnp.einsum(
        "kmn,kmr->knr", right_grad, right_proj_all, preferred_element_type=f32
    )
    down_sub_part = jnp.einsum("mn,mr->nr", down_grad, down_proj_all, preferred_element_type=f32)
    right_parts = jnp.concatenate([right_sub_part, down_sub_part[None]], axis=0)
    right_sub = exchange_sum(split_at(right_parts, 1, n_shard), "shard")
    right_update = galore_scale * jnp.einsum(
        "kmr,knr->kmn", right_dir_all, right_basis, preferred_element_type=f32
    )
    down_update = galore_scale * jnp.einsum(
        "mr,nr->mn", down_dir_all, down_basis, preferred_element_type=f32
    )

    lane_sub = [
        jnp.einsum("mn,rn->mr", left_grad[0], proj_all[0][:, :columns], preferred_element_type=f32),
        jnp.einsum("mn,rn->mr", left_grad[1], proj_all[0][:, columns:], preferred_element_type=f32),
        jnp.einsum("mn,rn->mr", gate_pieces[0], proj_all[1], preferred_element_type=f32),
        jnp.einsum("mn,rn->mr", gate_pieces[1], proj_all[2], preferred_element_type=f32),
    ]
    lane_sub = [
        jnp.dot(sub, lane.astype(f32), precision=highest)
        for sub, lane in zip(lane_sub, (lanes[0], lanes[0], lanes[1], lanes[2]))
    ]
    left_sub_part = jnp.stack([lane_sub[0], lane_sub[1], lane_sub[2] + lane_sub[3]])
    left_sub = swap_sum(split_at(left_sub_part, 1, n_tensor), "tensor", n_tensor)
    subspace = jnp.concatenate([left_sub, right_sub], axis=0)
    count = subspace.shape[0]
    gram_part = jnp.einsum("kir,kis->krs", subspace, subspace, precision=highest)
    gram_parts = gram_part.reshape(n_tensor, n_shard, -1, rank_width)
    gram_block = exchange_sum(swap_sum(gram_parts, "tensor", n_tensor), "shard")
    spread = lax.all_to_all(
        jnp.broadcast_to(gram_block.astype(bf16)[None], (n_shard,) + gram_block.shape),
        "shard",
        0,
        0,
    )
    gram_raw = lax.all_gather(spread, "tensor", axis=0, tiled=False)
    gram_raw = gram_raw.reshape(count, rank_width, rank_width).astype(f32)
    identity = jnp.eye(rank_width, dtype=f32)
    sum_squares = jnp.sum(gram_raw * identity, axis=(1, 2))
    gram_matrix = gram_raw / sum_squares[:, None, None]
    mixing = identity
    for turn_index in range(NSITER):
        factor = 1.5 * identity - 0.5 * gram_matrix
        if turn_index == 0:
            mixing = factor
        else:
            mixing = batch_product(mixing, factor)
        if turn_index + 1 < NSITER:
            gram_matrix = batch_product(batch_product(factor, factor), gram_matrix)
    normed = subspace / jnp.sqrt(sum_squares)[:, None, None]
    refreshed = batch_product(normed, mixing).astype(bf16)

    left_update = galore_scale * jnp.stack(
        [
            jnp.dot(left_lane_basis[0], dir_all[0][:, :columns], preferred_element_type=f32),
            jnp.dot(left_lane_basis[1], dir_all[0][:, columns:], preferred_element_type=f32),
        ]
    )
    gate_update = galore_scale * jnp.concatenate(
        [
            jnp.dot(gate_lane_basis[0], dir_all[1], preferred_element_type=f32),
            jnp.dot(gate_lane_basis[1], dir_all[2], preferred_element_type=f32),
        ],
        axis=1,
    )
    attn_update = jnp.take(jnp.concatenate([left_update, right_update], axis=0), inverse, axis=0)
    norm_first_new, norm_second_new, norm_direction = adam_moments(
        norm_grad, norm_first, norm_second, step_float
    )
    norm_param_new = norm_param - norm_rate * (norm_direction + weight_decay * norm_param)
    return (
        attn_update,
        gate_update,
        down_update,
        left_first_new,
        left_second_new,
        right_first_new,
        right_second_new,
        gate_first_new,
        gate_second_new,
        down_first_new,
        down_second_new,
        refreshed[0:2],
        refreshed[3:5][:, None],
        refreshed[2],
        refreshed[5][None],
        norm_param_new,
        norm_first_new,
        norm_second_new,
    )


def solution(mesh):
    in_specs = (
        P(),
        P(),
        P(None, "shard", "tensor"),
        P("shard", "tensor"),
        P("shard", "tensor"),
        P(None, "shard", None),
        P(None, "tensor", None),
        P("shard", None),
        P("tensor", None),
        P(None, "shard", "tensor"),
        P(None, "shard", "tensor"),
        P(None, "shard", "tensor"),
        P(None, "shard", "tensor"),
        P("shard", "tensor"),
        P("shard", "tensor"),
        P("shard", "tensor"),
        P("shard", "tensor"),
        P(None, ("shard", "tensor")),
        P(None, ("shard", "tensor")),
        P(None, ("shard", "tensor")),
        P(None, ("shard", "tensor")),
    )
    out_specs = (
        P(None, "shard", "tensor"),
        P("shard", "tensor"),
        P("shard", "tensor"),
        P(None, "shard", "tensor"),
        P(None, "shard", "tensor"),
        P(None, "shard", "tensor"),
        P(None, "shard", "tensor"),
        P("shard", "tensor"),
        P("shard", "tensor"),
        P("shard", "tensor"),
        P("shard", "tensor"),
        P(None, ("shard", "tensor"), None),
        P(None, "tensor", "shard", None),
        P(("shard", "tensor"), None),
        P("tensor", "shard", None),
        P(None, ("shard", "tensor")),
        P(None, ("shard", "tensor")),
        P(None, ("shard", "tensor")),
    )
    return jax.shard_map(
        functools.partial(body, mesh.shape["shard"], mesh.shape["tensor"]),
        mesh=mesh, in_specs=in_specs, out_specs=out_specs, check_vma=False)
```

```python
import functools

import jax
import jax.numpy as jnp
from jax import lax
from jax.sharding import PartitionSpec as P

NSITER = 5


highest = lax.Precision.HIGHEST
beta_one = 0.9
beta_two = 0.999
adam_eps = 1e-08
galore_scale = 0.25
norm_rate = 0.001
weight_decay = 0.1


def adam_moments(gradient, first_moment, second_moment, step_float):
    first_new = beta_one * first_moment + (1.0 - beta_one) * gradient
    second_new = beta_two * second_moment + (1.0 - beta_two) * gradient * gradient
    corr_first = 1.0 - beta_one**step_float
    corr_second = 1.0 - beta_two**step_float
    direction = first_new / corr_first / (jnp.sqrt(second_new / corr_second) + adam_eps)
    return (first_new, second_new, direction)


def batch_product(first_factor, second_factor):
    return jnp.einsum("kij,kjl->kil", first_factor, second_factor, precision=highest)


def swap_sum(parts, axis_name, size):
    if size == 1:
        return parts[0]
    if size == 2:
        own = lax.axis_index(axis_name)
        mine = lax.dynamic_index_in_dim(parts, own, 0, keepdims=False)
        other = lax.dynamic_index_in_dim(parts, 1 - own, 0, keepdims=False)
        return mine + lax.ppermute(other, axis_name, [(0, 1), (1, 0)])
    return jnp.sum(lax.all_to_all(parts, axis_name, 0, 0), axis=0)


def exchange_sum(parts, axis_name):
    received = lax.all_to_all(parts.astype(jnp.bfloat16), axis_name, 0, 0)
    return jnp.sum(received.astype(jnp.float32), axis=0)


def lane_matrix(order, count, block, axis_name):
    place = lax.iota(jnp.int32, count)
    relative = jnp.zeros_like(place)
    for level, bit in enumerate(order):
        relative = relative | (((place >> (len(order) - 1 - level)) & 1) << bit)
    start = (lax.axis_index(axis_name) ^ relative) * block
    target = (start[:, None] + lax.iota(jnp.int32, block)[None]).reshape(count * block, 1)
    return (target == lax.iota(jnp.int32, count * block)[None]).astype(jnp.bfloat16)


def partners(bit, count):
    return [(index, index ^ (1 << bit)) for index in range(count)]


def reduce_level(parts, orders, level, count, axis_name, others):
    halves = [part.shape[0] // 2 for part in parts]
    received = [
        lax.ppermute(part[half:].astype(jnp.bfloat16), axis_name, partners(order[level], count))
        for part, half, order in zip(parts, halves, orders)
    ]
    received, others = lax.optimization_barrier((received, others))
    parts = [
        part[:half] + other.astype(jnp.float32)
        for part, half, other in zip(parts, halves, received)
    ]
    return parts, others


def lane_gather(block, order, count, axis_name):
    for bit in reversed(order[1:]):
        other = lax.ppermute(block, axis_name, partners(bit, count))
        block = jnp.concatenate([block, other], axis=0)
    return block, lax.ppermute(block, axis_name, partners(order[0], count))


def lane_subspace(gradient, halves, lane):
    subs = [
        jnp.einsum("mn,rn->mr", gradient, half, preferred_element_type=jnp.float32)
        for half in halves
    ]
    return jnp.dot(jnp.concatenate(subs, axis=1), lane.astype(jnp.float32), precision=highest)


def lane_update(basis, halves):
    width = halves[0].shape[0]
    return jnp.dot(
        basis[:, :width], halves[0], preferred_element_type=jnp.float32
    ) + jnp.dot(basis[:, width:], halves[1], preferred_element_type=jnp.float32)


def split_at(array, axis, count):
    shape = array.shape[:axis] + (count, array.shape[axis] // count) + array.shape[axis + 1 :]
    return jnp.moveaxis(array.reshape(shape), axis, 0)


def body(
    n_shard,
    n_tensor,
    step_count,
    attn_side,
    attn_grad,
    gate_grad,
    down_grad,
    left_basis,
    right_basis,
    gate_basis,
    down_basis,
    left_first,
    left_second,
    right_first,
    right_second,
    gate_first,
    gate_second,
    down_first,
    down_second,
    norm_param,
    norm_grad,
    norm_first,
    norm_second,
):
    step_float = step_count[0].astype(jnp.float32)
    ordering = jnp.argsort(attn_side, stable=True)
    inverse = jnp.argsort(ordering, stable=True)
    picked = jnp.take(attn_grad, ordering, axis=0)
    left_grad = picked[:2]
    right_grad = picked[2:]
    bf16 = jnp.bfloat16
    f32 = jnp.float32
    columns = left_grad.shape[2]
    rank_width = gate_basis.shape[1]
    block = rank_width // n_shard
    bits = list(range(n_shard.bit_length() - 1))
    orders = (bits[2:] + bits[:2], bits, bits[1::-1] + bits[2:])
    lanes = [lane_matrix(order, n_shard, block, "shard") for order in orders]
    gate_columns = gate_grad.shape[1]
    cut = max(gate_columns // 256 * 128, 1)
    gate_pieces = (gate_grad[:, :cut], gate_grad[:, cut:])
    left_lane_basis = jnp.einsum("kmr,pr->kmp", left_basis, lanes[0])
    gate_lane_basis = [jnp.einsum("mr,pr->mp", gate_basis, lane) for lane in lanes[1:]]
    parts = [
        jnp.concatenate(
            [
                jnp.dot(left_lane_basis[0].T, left_grad[0], preferred_element_type=f32),
                jnp.dot(left_lane_basis[1].T, left_grad[1], preferred_element_type=f32),
            ],
            axis=1,
        ),
        jnp.dot(gate_lane_basis[0].T, gate_pieces[0], preferred_element_type=f32),
        jnp.dot(gate_lane_basis[1].T, gate_pieces[1], preferred_element_type=f32),
    ]
    right_part = jnp.einsum("kmn,knr->kmr", right_grad, right_basis, preferred_element_type=f32)
    down_part = jnp.dot(down_grad, down_basis, preferred_element_type=f32)
    levels = len(bits)
    summed, (right_part, down_part) = reduce_level(
        parts, orders, 0, n_shard, "shard", (right_part, down_part)
    )
    right_projected = swap_sum(split_at(right_part, 2, n_tensor), "tensor", n_tensor)
    down_projected = swap_sum(split_at(down_part, 1, n_tensor), "tensor", n_tensor)
    summed, (right_projected, down_projected) = reduce_level(
        summed, orders, 1, n_shard, "shard", (right_projected, down_projected)
    )
    right_proj_all = lax.all_gather(right_projected.astype(bf16), "tensor", axis=2, tiled=True)
    down_proj_all = lax.all_gather(down_projected.astype(bf16), "tensor", axis=1, tiled=True)
    for level in range(2, levels):
        summed, (right_proj_all, down_proj_all, right_projected, down_projected) = reduce_level(
            summed,
            orders,
            level,
            n_shard,
            "shard",
            (right_proj_all, down_proj_all, right_projected, down_projected),
        )
    proj_all = [
        lane_gather(piece.astype(bf16), order, n_shard, "shard")
        for piece, order in zip(summed, orders)
    ]
    left_projected = jnp.stack([summed[0][:, :columns], summed[0][:, columns:]])
    gate_projected = jnp.concatenate(summed[1:], axis=1)
    left_first_new, left_second_new, left_direction = adam_moments(
        left_projected, left_first, left_second, step_float
    )
    gate_first_new, gate_second_new, gate_direction = adam_moments(
        gate_projected, gate_first, gate_second, step_float
    )
    directions = [
        jnp.concatenate([left_direction[0].astype(bf16), left_direction[1].astype(bf16)], axis=1),
        gate_direction[:, :cut].astype(bf16),
        gate_direction[:, cut:].astype(bf16),
    ]
    dir_all = [
        lane_gather(piece, order, n_shard, "shard") for piece, order in zip(directions, orders)
    ]

    right_first_new, right_second_new, right_direction = adam_moments(
        right_projected, right_first, right_second, step_float
    )
    down_first_new, down_second_new, down_direction = adam_moments(
        down_projected, down_first, down_second, step_float
    )
    right_dir_all = lax.all_gather(right_direction.astype(bf16), "tensor", axis=2, tiled=True)
    down_dir_all = lax.all_gather(down_direction.astype(bf16), "tensor", axis=1, tiled=True)
    right_sub_part = jnp.einsum(
        "kmn,kmr->knr", right_grad, right_proj_all, preferred_element_type=f32
    )
    down_sub_part = jnp.einsum("mn,mr->nr", down_grad, down_proj_all, preferred_element_type=f32)
    right_parts = jnp.concatenate([right_sub_part, down_sub_part[None]], axis=0)
    right_sub = exchange_sum(split_at(right_parts, 1, n_shard), "shard")
    right_update = galore_scale * jnp.einsum(
        "kmr,knr->kmn", right_dir_all, right_basis, preferred_element_type=f32
    )
    down_update = galore_scale * jnp.einsum(
        "mr,nr->mn", down_dir_all, down_basis, preferred_element_type=f32
    )

    lane_sub = [
        lane_subspace(left_grad[0], [half[:, :columns] for half in proj_all[0]], lanes[0]),
        lane_subspace(left_grad[1], [half[:, columns:] for half in proj_all[0]], lanes[0]),
        lane_subspace(gate_pieces[0], proj_all[1], lanes[1]),
        lane_subspace(gate_pieces[1], proj_all[2], lanes[2]),
    ]
    left_sub_part = jnp.stack([lane_sub[0], lane_sub[1], lane_sub[2] + lane_sub[3]])
    left_sub = swap_sum(split_at(left_sub_part, 1, n_tensor), "tensor", n_tensor)
    subspace = jnp.concatenate([left_sub, right_sub], axis=0)
    count = subspace.shape[0]
    gram_part = jnp.einsum("kir,kis->krs", subspace, subspace, precision=highest)
    gram_parts = gram_part.reshape(n_tensor, n_shard, -1, rank_width)
    gram_block = exchange_sum(swap_sum(gram_parts, "tensor", n_tensor), "shard")
    spread = lax.all_to_all(
        jnp.broadcast_to(gram_block.astype(bf16)[None], (n_shard,) + gram_block.shape),
        "shard",
        0,
        0,
    )
    gram_raw = lax.all_gather(spread, "tensor", axis=0, tiled=False)
    gram_raw = gram_raw.reshape(count, rank_width, rank_width).astype(f32)
    identity = jnp.eye(rank_width, dtype=f32)
    sum_squares = jnp.sum(gram_raw * identity, axis=(1, 2))
    gram_matrix = gram_raw / sum_squares[:, None, None]
    mixing = identity
    for turn_index in range(NSITER):
        factor = 1.5 * identity - 0.5 * gram_matrix
        if turn_index == 0:
            mixing = factor
        else:
            mixing = batch_product(mixing, factor)
        if turn_index + 1 < NSITER:
            gram_matrix = batch_product(batch_product(factor, factor), gram_matrix)
    normed = subspace / jnp.sqrt(sum_squares)[:, None, None]
    refreshed = batch_product(normed, mixing).astype(bf16)

    left_update = galore_scale * jnp.stack(
        [
            lane_update(left_lane_basis[0], [half[:, :columns] for half in dir_all[0]]),
            lane_update(left_lane_basis[1], [half[:, columns:] for half in dir_all[0]]),
        ]
    )
    gate_update = galore_scale * jnp.concatenate(
        [
            lane_update(gate_lane_basis[0], dir_all[1]),
            lane_update(gate_lane_basis[1], dir_all[2]),
        ],
        axis=1,
    )
    attn_update = jnp.take(jnp.concatenate([left_update, right_update], axis=0), inverse, axis=0)
    norm_first_new, norm_second_new, norm_direction = adam_moments(
        norm_grad, norm_first, norm_second, step_float
    )
    norm_param_new = norm_param - norm_rate * (norm_direction + weight_decay * norm_param)
    return (
        attn_update,
        gate_update,
        down_update,
        left_first_new,
        left_second_new,
        right_first_new,
        right_second_new,
        gate_first_new,
        gate_second_new,
        down_first_new,
        down_second_new,
        refreshed[0:2],
        refreshed[3:5][:, None],
        refreshed[2],
        refreshed[5][None],
        norm_param_new,
        norm_first_new,
        norm_second_new,
    )


def solution(mesh):
    in_specs = (
        P(),
        P(),
        P(None, "shard", "tensor"),
        P("shard", "tensor"),
        P("shard", "tensor"),
        P(None, "shard", None),
        P(None, "tensor", None),
        P("shard", None),
        P("tensor", None),
        P(None, "shard", "tensor"),
        P(None, "shard", "tensor"),
        P(None, "shard", "tensor"),
        P(None, "shard", "tensor"),
        P("shard", "tensor"),
        P("shard", "tensor"),
        P("shard", "tensor"),
        P("shard", "tensor"),
        P(None, ("shard", "tensor")),
        P(None, ("shard", "tensor")),
        P(None, ("shard", "tensor")),
        P(None, ("shard", "tensor")),
    )
    out_specs = (
        P(None, "shard", "tensor"),
        P("shard", "tensor"),
        P("shard", "tensor"),
        P(None, "shard", "tensor"),
        P(None, "shard", "tensor"),
        P(None, "shard", "tensor"),
        P(None, "shard", "tensor"),
        P("shard", "tensor"),
        P("shard", "tensor"),
        P("shard", "tensor"),
        P("shard", "tensor"),
        P(None, ("shard", "tensor"), None),
        P(None, "tensor", "shard", None),
        P(("shard", "tensor"), None),
        P("tensor", "shard", None),
        P(None, ("shard", "tensor")),
        P(None, ("shard", "tensor")),
        P(None, ("shard", "tensor")),
    )
    return jax.shard_map(
        functools.partial(body, mesh.shape["shard"], mesh.shape["tensor"]),
        mesh=mesh, in_specs=in_specs, out_specs=out_specs, check_vma=False)
```

```python
import functools

import jax
import jax.numpy as jnp
from jax import lax
from jax.sharding import PartitionSpec as P

NSITER = 5


three_pass = lax.Precision.HIGH
beta_one = 0.9
beta_two = 0.999
adam_eps = 1e-08
galore_scale = 0.25
norm_rate = 0.001
weight_decay = 0.1


def adam_moments(gradient, first_moment, second_moment, step_float):
    first_new = beta_one * first_moment + (1.0 - beta_one) * gradient
    second_new = beta_two * second_moment + (1.0 - beta_two) * gradient * gradient
    corr_first = 1.0 - beta_one**step_float
    corr_second = 1.0 - beta_two**step_float
    direction = first_new / corr_first / (jnp.sqrt(second_new / corr_second) + adam_eps)
    return (first_new, second_new, direction)


def batch_product(first_factor, second_factor):
    return jnp.einsum("kij,kjl->kil", first_factor, second_factor, precision=three_pass)


def swap_sum(parts, axis_name, size):
    if size == 1:
        return parts[0]
    if size == 2:
        own = lax.axis_index(axis_name)
        mine = lax.dynamic_index_in_dim(parts, own, 0, keepdims=False)
        other = lax.dynamic_index_in_dim(parts, 1 - own, 0, keepdims=False)
        return mine + lax.ppermute(other, axis_name, [(0, 1), (1, 0)])
    return jnp.sum(lax.all_to_all(parts, axis_name, 0, 0), axis=0)


def exchange_sum(parts, axis_name):
    received = lax.all_to_all(parts.astype(jnp.bfloat16), axis_name, 0, 0)
    return jnp.sum(received.astype(jnp.float32), axis=0)


def lane_matrix(order, count, block, axis_name):
    place = lax.iota(jnp.int32, count)
    relative = jnp.zeros_like(place)
    for level, bit in enumerate(order):
        relative = relative | (((place >> (len(order) - 1 - level)) & 1) << bit)
    start = (lax.axis_index(axis_name) ^ relative) * block
    target = (start[:, None] + lax.iota(jnp.int32, block)[None]).reshape(count * block, 1)
    return (target == lax.iota(jnp.int32, count * block)[None]).astype(jnp.bfloat16)


def partners(bit, count):
    return [(index, index ^ (1 << bit)) for index in range(count)]


def reduce_level(parts, orders, level, count, axis_name, others):
    halves = [part.shape[0] // 2 for part in parts]
    received = [
        lax.ppermute(part[half:].astype(jnp.bfloat16), axis_name, partners(order[level], count))
        for part, half, order in zip(parts, halves, orders)
    ]
    received, others = lax.optimization_barrier((received, others))
    parts = [
        part[:half] + other.astype(jnp.float32)
        for part, half, other in zip(parts, halves, received)
    ]
    return parts, others


def lane_gather(block, order, count, axis_name):
    for bit in reversed(order[1:]):
        other = lax.ppermute(block, axis_name, partners(bit, count))
        block = jnp.concatenate([block, other], axis=0)
    return block, lax.ppermute(block, axis_name, partners(order[0], count))


def lane_subspace(gradient, halves, lane):
    subs = [
        jnp.einsum("mn,rn->mr", gradient, half, preferred_element_type=jnp.float32)
        for half in halves
    ]
    return jnp.dot(jnp.concatenate(subs, axis=1), lane.astype(jnp.float32), precision=three_pass)


def lane_update(basis, halves):
    width = halves[0].shape[0]
    return jnp.dot(
        basis[:, :width], halves[0], preferred_element_type=jnp.float32
    ) + jnp.dot(basis[:, width:], halves[1], preferred_element_type=jnp.float32)


def split_at(array, axis, count):
    shape = array.shape[:axis] + (count, array.shape[axis] // count) + array.shape[axis + 1 :]
    return jnp.moveaxis(array.reshape(shape), axis, 0)


def body(
    n_shard,
    n_tensor,
    step_count,
    attn_side,
    attn_grad,
    gate_grad,
    down_grad,
    left_basis,
    right_basis,
    gate_basis,
    down_basis,
    left_first,
    left_second,
    right_first,
    right_second,
    gate_first,
    gate_second,
    down_first,
    down_second,
    norm_param,
    norm_grad,
    norm_first,
    norm_second,
):
    step_float = step_count[0].astype(jnp.float32)
    ordering = jnp.argsort(attn_side, stable=True)
    inverse = jnp.argsort(ordering, stable=True)
    picked = jnp.take(attn_grad, ordering, axis=0)
    left_grad = picked[:2]
    right_grad = picked[2:]
    bf16 = jnp.bfloat16
    f32 = jnp.float32
    columns = left_grad.shape[2]
    rank_width = gate_basis.shape[1]
    block = rank_width // n_shard
    bits = list(range(n_shard.bit_length() - 1))
    orders = (bits[2:] + bits[:2], bits, bits[1::-1] + bits[2:])
    lanes = [lane_matrix(order, n_shard, block, "shard") for order in orders]
    gate_columns = gate_grad.shape[1]
    cut = max(gate_columns // 256 * 128, 1)
    gate_pieces = (gate_grad[:, :cut], gate_grad[:, cut:])
    left_lane_basis = jnp.einsum("kmr,pr->kmp", left_basis, lanes[0])
    gate_lane_basis = [jnp.einsum("mr,pr->mp", gate_basis, lane) for lane in lanes[1:]]
    parts = [
        jnp.concatenate(
            [
                jnp.dot(left_lane_basis[0].T, left_grad[0], preferred_element_type=f32),
                jnp.dot(left_lane_basis[1].T, left_grad[1], preferred_element_type=f32),
            ],
            axis=1,
        ),
        jnp.dot(gate_lane_basis[0].T, gate_pieces[0], preferred_element_type=f32),
        jnp.dot(gate_lane_basis[1].T, gate_pieces[1], preferred_element_type=f32),
    ]
    right_part = jnp.einsum("kmn,knr->kmr", right_grad, right_basis, preferred_element_type=f32)
    down_part = jnp.dot(down_grad, down_basis, preferred_element_type=f32)
    levels = len(bits)
    summed, (right_part, down_part) = reduce_level(
        parts, orders, 0, n_shard, "shard", (right_part, down_part)
    )
    right_projected = swap_sum(split_at(right_part, 2, n_tensor), "tensor", n_tensor)
    down_projected = swap_sum(split_at(down_part, 1, n_tensor), "tensor", n_tensor)
    summed, (right_projected, down_projected) = reduce_level(
        summed, orders, 1, n_shard, "shard", (right_projected, down_projected)
    )
    right_proj_all = lax.all_gather(right_projected.astype(bf16), "tensor", axis=2, tiled=True)
    down_proj_all = lax.all_gather(down_projected.astype(bf16), "tensor", axis=1, tiled=True)
    for level in range(2, levels):
        summed, (right_proj_all, down_proj_all, right_projected, down_projected) = reduce_level(
            summed,
            orders,
            level,
            n_shard,
            "shard",
            (right_proj_all, down_proj_all, right_projected, down_projected),
        )
    proj_all = [
        lane_gather(piece.astype(bf16), order, n_shard, "shard")
        for piece, order in zip(summed, orders)
    ]
    left_projected = jnp.stack([summed[0][:, :columns], summed[0][:, columns:]])
    gate_projected = jnp.concatenate(summed[1:], axis=1)
    left_first_new, left_second_new, left_direction = adam_moments(
        left_projected, left_first, left_second, step_float
    )
    gate_first_new, gate_second_new, gate_direction = adam_moments(
        gate_projected, gate_first, gate_second, step_float
    )
    directions = [
        jnp.concatenate([left_direction[0].astype(bf16), left_direction[1].astype(bf16)], axis=1),
        gate_direction[:, :cut].astype(bf16),
        gate_direction[:, cut:].astype(bf16),
    ]
    dir_all = [
        lane_gather(piece, order, n_shard, "shard") for piece, order in zip(directions, orders)
    ]

    right_first_new, right_second_new, right_direction = adam_moments(
        right_projected, right_first, right_second, step_float
    )
    down_first_new, down_second_new, down_direction = adam_moments(
        down_projected, down_first, down_second, step_float
    )
    right_dir_all = lax.all_gather(right_direction.astype(bf16), "tensor", axis=2, tiled=True)
    down_dir_all = lax.all_gather(down_direction.astype(bf16), "tensor", axis=1, tiled=True)
    right_sub_part = jnp.einsum(
        "kmn,kmr->knr", right_grad, right_proj_all, preferred_element_type=f32
    )
    down_sub_part = jnp.einsum("mn,mr->nr", down_grad, down_proj_all, preferred_element_type=f32)
    right_parts = jnp.concatenate([right_sub_part, down_sub_part[None]], axis=0)
    right_sub = exchange_sum(split_at(right_parts, 1, n_shard), "shard")
    right_update = galore_scale * jnp.einsum(
        "kmr,knr->kmn", right_dir_all, right_basis, preferred_element_type=f32
    )
    down_update = galore_scale * jnp.einsum(
        "mr,nr->mn", down_dir_all, down_basis, preferred_element_type=f32
    )

    lane_sub = [
        lane_subspace(left_grad[0], [half[:, :columns] for half in proj_all[0]], lanes[0]),
        lane_subspace(left_grad[1], [half[:, columns:] for half in proj_all[0]], lanes[0]),
        lane_subspace(gate_pieces[0], proj_all[1], lanes[1]),
        lane_subspace(gate_pieces[1], proj_all[2], lanes[2]),
    ]
    left_sub_part = jnp.stack([lane_sub[0], lane_sub[1], lane_sub[2] + lane_sub[3]])
    left_sub = swap_sum(split_at(left_sub_part, 1, n_tensor), "tensor", n_tensor)
    subspace = jnp.concatenate([left_sub, right_sub], axis=0)
    count = subspace.shape[0]
    gram_part = jnp.einsum("kir,kis->krs", subspace, subspace, precision=three_pass)
    gram_parts = gram_part.reshape(n_tensor, n_shard, -1, rank_width)
    gram_block = exchange_sum(swap_sum(gram_parts, "tensor", n_tensor), "shard")
    spread = lax.all_to_all(
        jnp.broadcast_to(gram_block.astype(bf16)[None], (n_shard,) + gram_block.shape),
        "shard",
        0,
        0,
    )
    gram_raw = lax.all_gather(spread, "tensor", axis=0, tiled=False)
    gram_raw = gram_raw.reshape(count, rank_width, rank_width).astype(f32)
    identity = jnp.eye(rank_width, dtype=f32)
    sum_squares = jnp.sum(gram_raw * identity, axis=(1, 2))
    gram_matrix = gram_raw / sum_squares[:, None, None]
    mixing = identity
    for turn_index in range(NSITER):
        factor = 1.5 * identity - 0.5 * gram_matrix
        if turn_index == 0:
            mixing = factor
        else:
            mixing = batch_product(mixing, factor)
        if turn_index + 1 < NSITER:
            gram_matrix = batch_product(batch_product(factor, factor), gram_matrix)
    normed = subspace / jnp.sqrt(sum_squares)[:, None, None]
    refreshed = batch_product(normed, mixing).astype(bf16)

    left_update = galore_scale * jnp.stack(
        [
            lane_update(left_lane_basis[0], [half[:, :columns] for half in dir_all[0]]),
            lane_update(left_lane_basis[1], [half[:, columns:] for half in dir_all[0]]),
        ]
    )
    gate_update = galore_scale * jnp.concatenate(
        [
            lane_update(gate_lane_basis[0], dir_all[1]),
            lane_update(gate_lane_basis[1], dir_all[2]),
        ],
        axis=1,
    )
    attn_update = jnp.take(jnp.concatenate([left_update, right_update], axis=0), inverse, axis=0)
    norm_first_new, norm_second_new, norm_direction = adam_moments(
        norm_grad, norm_first, norm_second, step_float
    )
    norm_param_new = norm_param - norm_rate * (norm_direction + weight_decay * norm_param)
    return (
        attn_update,
        gate_update,
        down_update,
        left_first_new,
        left_second_new,
        right_first_new,
        right_second_new,
        gate_first_new,
        gate_second_new,
        down_first_new,
        down_second_new,
        refreshed[0:2],
        refreshed[3:5][:, None],
        refreshed[2],
        refreshed[5][None],
        norm_param_new,
        norm_first_new,
        norm_second_new,
    )


def solution(mesh):
    in_specs = (
        P(),
        P(),
        P(None, "shard", "tensor"),
        P("shard", "tensor"),
        P("shard", "tensor"),
        P(None, "shard", None),
        P(None, "tensor", None),
        P("shard", None),
        P("tensor", None),
        P(None, "shard", "tensor"),
        P(None, "shard", "tensor"),
        P(None, "shard", "tensor"),
        P(None, "shard", "tensor"),
        P("shard", "tensor"),
        P("shard", "tensor"),
        P("shard", "tensor"),
        P("shard", "tensor"),
        P(None, ("shard", "tensor")),
        P(None, ("shard", "tensor")),
        P(None, ("shard", "tensor")),
        P(None, ("shard", "tensor")),
    )
    out_specs = (
        P(None, "shard", "tensor"),
        P("shard", "tensor"),
        P("shard", "tensor"),
        P(None, "shard", "tensor"),
        P(None, "shard", "tensor"),
        P(None, "shard", "tensor"),
        P(None, "shard", "tensor"),
        P("shard", "tensor"),
        P("shard", "tensor"),
        P("shard", "tensor"),
        P("shard", "tensor"),
        P(None, ("shard", "tensor"), None),
        P(None, "tensor", "shard", None),
        P(("shard", "tensor"), None),
        P("tensor", "shard", None),
        P(None, ("shard", "tensor")),
        P(None, ("shard", "tensor")),
        P(None, ("shard", "tensor")),
    )
    return jax.shard_map(
        functools.partial(body, mesh.shape["shard"], mesh.shape["tensor"]),
        mesh=mesh, in_specs=in_specs, out_specs=out_specs, check_vma=False)
```
